32 devices in a mesh: seq: 8 (over z, x), head: 4 (over y, core).
Axes of the slice: x: 2, y: 2, z: 4, core: 2. Of those that a mesh axis runs over, the one named last changes fastest.
Arguments:
- scaled_input: bfloat16 [8192, 8192], P('seq', 'head'), may hold values from -0.059814453 to 0.059814453
- out_grad: bfloat16 [8192, 8192], P('seq', 'head'), may hold values from -1.796875 to 1.796875
- write_proj: bfloat16 [8192, 128], P('seq'), may hold values from -0.5 to 0.5
- read_proj: bfloat16 [8192, 128], P('seq'), may hold values from -0.5 to 0.5
- log_decay: float32 [128, 8192], P('head', 'seq'), may hold values from -0.8 to 0, as said below
Outputs:
- grad_input: bfloat16 [8192, 8192], P('seq', 'head')
- grad_write: bfloat16 [8192, 128], P(('seq', 'head'))
- grad_read: bfloat16 [8192, 128], P(('seq', 'head'))
The draws below stay inside these ranges and needn't reach their ends.
Inputs may be any that keep to these rules, and one draw needn't show every extreme that they name: `log_decay`: logarithms of the per-token decays of each head.
All inputs are finite; a program needn't handle non-finite values.
Results may differ from the reference program's by a relative error of at most 0.0045.
Values sent between devices are 32-bit elements; how exact they have to be, the bound alone decides.
A program may use at most 192 MiB of HBM per device.

```python
import math
import jax
import jax.numpy as jnp
from jax import lax

HEAD_DIM = 64
STATE = 128
BLOCK = 256
TOK_DEV = 1024
HEADS = 128
INNER = 8192
SEGMENT_TOKENS = 8192


def draw_log_decay(key, part):
    random_subkeys = [jax.random.fold_in(key, 11 + offset) for offset in range(8)]
    quick_share = 8
    quick_heads = jax.random.randint(random_subkeys[0], (HEADS,), 0, 16) < quick_share
    slow_rate = jax.random.uniform(random_subkeys[1], (HEADS,), jnp.float32, 0.1, 0.4) / SEGMENT_TOKENS
    quick_rate = jnp.exp(jax.random.uniform(random_subkeys[2], (HEADS,), jnp.float32, math.log(1.0 / 50.0), math.log(1.0 / 30.0)))
    decay_factors = jnp.where(quick_heads, quick_rate, slow_rate)
    split_multiplier = jnp.exp(jax.random.uniform(random_subkeys[3], (HEADS, SEGMENT_TOKENS // TOK_DEV), jnp.float32, math.log(0.5), math.log(2.0)))
    split_multiplier = jnp.repeat(split_multiplier, TOK_DEV, axis=1, total_repeat_length=SEGMENT_TOKENS)
    jaggedness_level = jax.random.uniform(random_subkeys[4], (HEADS, SEGMENT_TOKENS), jnp.float32, 0.5, 1.5)
    leading_spike = jax.random.randint(random_subkeys[5], (), 0, SEGMENT_TOKENS)
    trailing_spike = (leading_spike + jax.random.randint(random_subkeys[6], (), 1, SEGMENT_TOKENS)) % SEGMENT_TOKENS
    spike_values = jnp.stack([leading_spike, trailing_spike])
    loss_values = jax.random.uniform(random_subkeys[7], (2,), jnp.float32, 0.2, 0.5)
    token_positions = jnp.arange(SEGMENT_TOKENS)
    spike_logarithm = jnp.sum(jnp.where(token_positions[None, :] == spike_values[:, None], jnp.log(1.0 - loss_values)[:, None], 0.0), axis=0)
    return -decay_factors[:, None] * split_multiplier * jaggedness_level + spike_logarithm[None, :]


def strengthened(drawn, own_key, source, target, parts, factor):
    owner, partner = [(jnp.arange(drawn.shape[position]) // (drawn.shape[position] // parts)).reshape([-1 if axis == position else 1 for axis in range(drawn.ndim)]) for position in (source, target)]
    chosen = jax.random.permutation(own_key, parts)[partner]
    strong = (owner == chosen) | (owner == (partner + parts // 2) % parts)
    return jnp.where(strong, factor * drawn, drawn)


def block_scale(key, dims, cuts, least, largest):
    loudness = 1.0
    for position, shards_of in cuts:
        steps = jax.random.uniform(jax.random.fold_in(jax.random.fold_in(key, 6), position), (shards_of,), jnp.float32, least / len(cuts), largest / len(cuts))
        loudness = loudness * jnp.repeat(jnp.exp(steps), dims[position] // shards_of).reshape((-1,) + (1,) * (len(dims) - 1 - position))
    return loudness


def scatter_about(key, extent, width, limit, shards=(), dtype=jnp.bfloat16):
    entries = width * jax.random.normal(key, extent, jnp.float32)
    if shards:
        entries = entries * block_scale(key, extent, shards, -0.22, 0.18)
    return jnp.clip(entries, -limit, limit).astype(dtype)


def bell_draw_with(key, shape, scale, most, cuts, heavy, kind=jnp.bfloat16):
    result = scale * jax.random.normal(key, shape, jnp.float32)
    if cuts:
        result = result * block_scale(key, shape, cuts, -0.22, 0.18)
    return jnp.clip(strengthened(result, jax.random.fold_in(key, 3), *heavy), -most, most).astype(kind)


def setup_inputs(seed: int = 0) -> dict:
    key_list = jax.random.split(jax.random.key(seed), 6)
    return {
        "scaled_input": scatter_about(key_list[0], (SEGMENT_TOKENS, INNER), 0.01, 0.059814453, ((0, 8), (1, 4))),
        "out_grad": bell_draw_with(key_list[1], (SEGMENT_TOKENS, INNER), 0.3, 1.796875, ((0, 8), (1, 4)), (1, 0, 8, 2.0)),
        "write_proj": scatter_about(key_list[2], (SEGMENT_TOKENS, STATE), STATE ** -0.5, 0.5, ((0, 8),)),
        "read_proj": scatter_about(key_list[3], (SEGMENT_TOKENS, STATE), STATE ** -0.5, 0.5, ((0, 8),)),
        "log_decay": draw_log_decay(jax.random.fold_in(key_list[5], 71), 0),
    }


highest = lax.Precision.HIGHEST


def block_terms(inputs, grads, writes, reads, cumulative, entering, leaving):
    length = cumulative.shape[1]
    token_positions = jnp.arange(length)
    upper = token_positions[None, :] >= token_positions[:, None]
    spread = cumulative[:, None, :] - cumulative[:, :, None]
    decay_mat = jnp.exp(jnp.where(upper[None], spread, -jnp.inf))
    inputs_f = inputs.astype(jnp.float32)
    grads_f = grads.astype(jnp.float32)
    writes_f = writes.astype(jnp.float32)
    reads_f = reads.astype(jnp.float32)
    to_end = jnp.exp(cumulative[:, -1:] - cumulative)
    from_start = jnp.exp(cumulative)
    pairs = jnp.dot(writes, reads.T, preferred_element_type=jnp.float32)
    weights_x = (decay_mat * pairs[None]).astype(jnp.bfloat16)
    weights_x = lax.optimization_barrier(weights_x).astype(jnp.float32)
    intra = jnp.einsum('hij,jhp->ihp', weights_x, grads_f, precision=highest)
    inter = to_end.T[:, :, None] * jnp.einsum('in,hnp->ihp', writes_f, leaving, precision=highest)
    grad_input = (intra + inter).astype(jnp.bfloat16).reshape(length, -1)
    cross = jnp.einsum('ihp,jhp->hij', inputs_f, grads_f, precision=highest)
    weights_w = (decay_mat * cross).astype(jnp.bfloat16)
    weights_w = lax.optimization_barrier(weights_w).astype(jnp.float32)
    scaled_in = to_end.T[:, :, None] * inputs_f
    scaled_grad = from_start.T[:, :, None] * grads_f
    part_write = jnp.einsum('hij,jn->in', weights_w, reads_f, precision=highest) + jnp.einsum('ihp,hnp->in', scaled_in, leaving, precision=highest)
    part_read = jnp.einsum('hij,in->jn', weights_w, writes_f, precision=highest) + jnp.einsum('jhp,hnp->jn', scaled_grad, entering, precision=highest)
    return grad_input, part_write, part_read


def reference(scaled_input, out_grad, write_proj, read_proj, log_decay):
    count = SEGMENT_TOKENS // BLOCK
    inputs = scaled_input.reshape(count, BLOCK, HEADS, HEAD_DIM)
    grads = out_grad.reshape(count, BLOCK, HEADS, HEAD_DIM)
    writes = write_proj.reshape(count, BLOCK, STATE)
    reads = read_proj.reshape(count, BLOCK, STATE)
    cumulative = jnp.cumsum(log_decay.reshape(HEADS, count, BLOCK), axis=2).transpose(1, 0, 2)

    def forward(carried, pieces):
        block_in, block_write, block_cum = pieces
        to_end = jnp.exp(block_cum[:, -1:] - block_cum)
        scaled = to_end.T[:, :, None] * block_in.astype(jnp.float32)
        local = jnp.einsum('in,ihp->hnp', block_write.astype(jnp.float32), scaled, precision=highest)
        return jnp.exp(block_cum[:, -1])[:, None, None] * carried + local, carried

    def backward(carried, pieces):
        block_grad, block_read, block_cum = pieces
        scaled = jnp.exp(block_cum).T[:, :, None] * block_grad.astype(jnp.float32)
        local = jnp.einsum('in,ihp->hnp', block_read.astype(jnp.float32), scaled, precision=highest)
        return jnp.exp(block_cum[:, -1])[:, None, None] * carried + local, carried

    start = jnp.zeros((HEADS, STATE, HEAD_DIM), jnp.float32)
    entering = lax.scan(forward, start, (inputs, writes, cumulative))[1]
    leaving = lax.scan(backward, start, (grads, reads, cumulative), reverse=True)[1]
    results = lax.map(lambda pieces: block_terms(*pieces), (inputs, grads, writes, reads, cumulative, entering, leaving))
    grad_input = results[0].reshape(SEGMENT_TOKENS, INNER)
    grad_write = results[1].reshape(SEGMENT_TOKENS, STATE).astype(jnp.bfloat16)
    grad_read = results[2].reshape(SEGMENT_TOKENS, STATE).astype(jnp.bfloat16)
    return (grad_input, grad_write, grad_read)
```

```python
import functools
import jax
import jax.numpy as jnp
from jax import lax
from jax.experimental import pallas as pl
from jax.experimental.pallas import tpu as pltpu
from jax.sharding import PartitionSpec as P

TILE = 128
MID = TILE // 2 - 1
CHUNK = 8
MESH = pl.DeviceIdType.MESH
F32 = jnp.float32
BF16 = jnp.bfloat16


def dot(a, b, ca, cb):
    return lax.dot_general(a, b, (((ca,), (cb,)), ((), ())), preferred_element_type=F32)


def pieces(value, count, axis):
    parts = []
    for _ in range(count):
        part = value.astype(BF16)
        parts.append(part)
        value = value - part.astype(F32)
    return jnp.concatenate(parts, axis=axis)


def fill_expand(expand_ref, heads):
    rows, width = expand_ref.shape
    size = width // heads
    row = lax.broadcasted_iota(jnp.int32, (rows, width), 0)
    col = lax.broadcasted_iota(jnp.int32, (rows, width), 1)
    low = (row % heads) * size
    expand_ref[...] = jnp.where((col >= low) & (col < low + size), 1.0, 0.0).astype(BF16)


def decays(logs):
    row = lax.broadcasted_iota(jnp.int32, (TILE, TILE), 0)
    col = lax.broadcasted_iota(jnp.int32, (TILE, TILE), 1)
    rel = jnp.where(col <= row, 1.0, 0.0) - jnp.where(col <= MID, 1.0, 0.0)
    row8 = lax.broadcasted_iota(jnp.int32, (8, TILE), 0)
    col8 = lax.broadcasted_iota(jnp.int32, (8, TILE), 1)
    first = (col8 <= MID) & (row8 != 1)
    last = (col8 > MID) & (row8 != 0)
    ends = jnp.where(first | last, 1.0, 0.0)
    parts = pieces(logs, 3, 1)
    rel = rel.astype(BF16)
    ends = ends.astype(BF16)
    rel = dot(jnp.concatenate([rel] * 3, 1), parts, 1, 1)
    ends = dot(jnp.concatenate([ends] * 3, 1), parts, 1, 1)
    return rel, ends


def spread(value, expand_ref):
    return dot(pieces(value, 2, 1), expand_ref[...], 1, 0)


def summary_kernel(heads, x_ref, g_ref, w_ref, r_ref, ld_ref, state_ref, decay_ref, expand_ref):
    k = pl.program_id(0)

    @pl.when(k == 0)
    def _():
        fill_expand(expand_ref, heads)
        state_ref[...] = jnp.zeros_like(state_ref)
        decay_ref[...] = jnp.ones_like(decay_ref)

    rel, ends = decays(ld_ref[...])
    ends = spread(jnp.exp(ends), expand_ref)
    from_start, to_end, whole = ends[0:1], ends[1:2], ends[2:3]
    xs = (x_ref[...].astype(F32) * spread(jnp.exp(-rel), expand_ref)).astype(BF16)
    gs = (g_ref[...].astype(F32) * spread(jnp.exp(rel), expand_ref)).astype(BF16)
    before = decay_ref[0:1]
    state_ref[0] = whole * state_ref[0] + to_end * dot(w_ref[...], xs, 0, 0)
    state_ref[1] += (before * from_start) * dot(r_ref[...], gs, 0, 0)
    decay_ref[...] = decay_ref[...] * whole


def chain_kernel(state_ref, decay_ref, out_ref, got, prior, passed, theirs, dec,
                 sa, ra, sb, rb, sc, rc, sd, rd):
    me = lax.axis_index("seq")
    count = lax.axis_size("seq")
    odd = lax.rem(me, 2)
    partner = me + 1 - 2 * odd
    step = 4 * odd - 2
    nxt, prv = me + step, me - step
    has_next = (nxt >= 0) & (nxt < count)
    has_prev = (prv >= 0) & (prv < count)
    fed = partner + step
    partner_prev = (fed >= 0) & (fed < count)
    mine, other = 1 - odd, odd
    barrier = pltpu.get_barrier_semaphore()
    pl.semaphore_signal(barrier, 1, device_id={"seq": partner}, device_id_type=MESH)

    @pl.when(has_next)
    def _():
        pl.semaphore_signal(barrier, 1, device_id={"seq": nxt}, device_id_type=MESH)

    @pl.when(has_prev)
    def _():
        pl.semaphore_signal(barrier, 1, device_id={"seq": prv}, device_id_type=MESH)

    peers = 1 + has_next.astype(jnp.int32) + has_prev.astype(jnp.int32)
    pl.semaphore_wait(barrier, peers)
    chunks = state_ref.shape[1] // CHUNK

    def rows(c):
        return pl.ds(c * CHUNK, CHUNK)

    def swap(c):
        return pltpu.make_async_remote_copy(
            state_ref.at[other, rows(c)], got.at[rows(c)], sa.at[c], ra.at[c],
            device_id={"seq": partner}, device_id_type=MESH)

    def forward(c):
        return pltpu.make_async_remote_copy(
            passed.at[rows(c)], prior.at[rows(c)], sb.at[c], rb.at[c],
            device_id={"seq": nxt}, device_id_type=MESH)

    def hand(c):
        return pltpu.make_async_remote_copy(
            prior.at[rows(c)], theirs.at[rows(c)], sc.at[c], rc.at[c],
            device_id={"seq": partner}, device_id_type=MESH)

    ratio = pltpu.make_async_remote_copy(
        decay_ref, dec, sd, rd, device_id={"seq": partner}, device_id_type=MESH)
    ratio.start()
    for c in range(chunks):
        swap(c).start()
    ratio.wait_recv()
    own = decay_ref[0:1]
    partners = dec[0:1]
    pair = own * partners
    for c in range(chunks):
        swap(c).wait_recv()
        summed = own * got[rows(c)] + state_ref[mine, rows(c)]

        @pl.when(has_prev)
        def _():
            forward(c).wait_recv()
            hand(c).start()
            passed[rows(c)] = pair * prior[rows(c)] + summed
            out_ref[0, rows(c)] = partners * prior[rows(c)] + got[rows(c)]

        @pl.when(jnp.logical_not(has_prev))
        def _():
            passed[rows(c)] = summed
            out_ref[0, rows(c)] = got[rows(c)]

        @pl.when(has_next)
        def _():
            forward(c).start()

    for c in range(chunks):

        @pl.when(partner_prev)
        def _():
            hand(c).wait_recv()
            out_ref[1, rows(c)] = theirs[rows(c)]

        @pl.when(jnp.logical_not(partner_prev))
        def _():
            out_ref[1, rows(c)] = jnp.zeros_like(theirs[rows(c)])

    ratio.wait_send()
    for c in range(chunks):
        swap(c).wait_send()

        @pl.when(has_prev)
        def _():
            hand(c).wait_send()

        @pl.when(has_next)
        def _():
            forward(c).wait_send()


def main_kernel(heads, tiles, x_ref, g_ref, w_ref, r_ref, ld_ref, in_ref, gi_ref, gw_ref, gr_ref,
                expand_ref, xs_ref, gs_ref, carry_ref):
    i = pl.program_id(0)
    odd = lax.rem(lax.axis_index("seq"), 2)

    @pl.when(i == 0)
    def _():
        fill_expand(expand_ref, heads)
        carry_ref[...] = in_ref[1 - odd]

    @pl.when(i == tiles)
    def _():
        carry_ref[...] = in_ref[odd]

    k = jnp.where(i < tiles, i, 2 * tiles - 1 - i)
    span = pl.ds(pl.multiple_of(k * TILE, TILE), TILE)
    rel, ends = decays(ld_ref[:, span])
    ends = spread(jnp.exp(ends), expand_ref)
    from_start, to_end, whole = ends[0:1], ends[1:2], ends[2:3]
    writes, reads = w_ref[span], r_ref[span]
    row = lax.broadcasted_iota(jnp.int32, (TILE, TILE), 0)
    col = lax.broadcasted_iota(jnp.int32, (TILE, TILE), 1)
    upper = col >= row

    @pl.when(i < tiles)
    def _():
        xs = (x_ref[...].astype(F32) * spread(jnp.exp(-rel), expand_ref)).astype(BF16)
        gs = (g_ref[...].astype(F32) * spread(jnp.exp(rel), expand_ref)).astype(BF16)
        xs_ref[span] = xs
        gs_ref[span] = gs
        weights = jnp.where(upper, dot(xs, gs, 1, 1), 0.0)
        high = weights.astype(BF16)
        entering = (from_start * carry_ref[...]).astype(BF16)
        gw_ref[span] = dot(high, reads, 1, 0)
        gr_ref[span] = dot(high, writes, 0, 0) + dot(gs, entering, 1, 1)
        carry_ref[...] = whole * carry_ref[...] + to_end * dot(writes, xs, 0, 0)

    @pl.when(i >= tiles)
    def _():
        xs = xs_ref[span]
        gs = gs_ref[span]
        leaving = (to_end * carry_ref[...]).astype(BF16)
        pairs = jnp.where(upper, dot(writes, reads, 1, 1), 0.0).astype(BF16)
        left = jnp.concatenate([pairs, writes], 1)
        right = jnp.concatenate([gs, leaving], 0)
        gi_ref[...] = (spread(jnp.exp(-rel), expand_ref) * dot(left, right, 1, 0)).astype(BF16)
        gw_ref[span] += dot(xs, leaving, 1, 1)
        carry_ref[...] = whole * carry_ref[...] + from_start * dot(reads, gs, 0, 0)


def scatter_kernel(gw_ref, gr_ref, ow_ref, or_ref, near, half, far, sa, ra, sb, rb):
    me = lax.axis_index("head")
    count = lax.axis_size("head")
    chips = count // 2
    core = lax.rem(me, 2)
    chip = me // 2
    mate = me + 1 - 2 * core
    size = ow_ref.shape[0]
    barrier = pltpu.get_barrier_semaphore()
    pl.semaphore_signal(barrier, 1, device_id={"head": mate}, device_id_type=MESH)
    for d in range(1, chips):
        there = 2 * lax.rem(chip + d, chips) + core
        pl.semaphore_signal(barrier, 1, device_id={"head": there}, device_id_type=MESH)
    pl.semaphore_wait(barrier, chips)

    def block(h):
        return pl.ds(pl.multiple_of(h * size, size), size)

    def swap(which, d):
        at = 2 * lax.rem(chip + d, chips) + 1 - core
        ref = (gw_ref, gr_ref)[which]
        return pltpu.make_async_remote_copy(
            ref.at[block(at)], near.at[which, d], sa.at[which, d], ra.at[which, d],
            device_id={"head": mate}, device_id_type=MESH)

    def cross(d):
        there = 2 * lax.rem(chip + d, chips) + core
        return pltpu.make_async_remote_copy(
            half.at[:, d], far.at[:, d], sb.at[d], rb.at[d],
            device_id={"head": there}, device_id_type=MESH)

    order = [d for d in range(1, chips)] + [0]
    for d in order:
        for which in range(2):
            swap(which, d).start()
    for d in order:
        at = 2 * lax.rem(chip + d, chips) + core
        for which, ref in enumerate((gw_ref, gr_ref)):
            swap(which, d).wait_recv()
            half[which, d] = near[which, d] + ref[block(at)]
        if d:
            cross(d).start()
    total = [half[0, 0], half[1, 0]]
    for d in range(1, chips):
        cross(d).wait_recv()
        total = [total[0] + far[0, d], total[1] + far[1, d]]
    ow_ref[...] = total[0].astype(BF16)
    or_ref[...] = total[1].astype(BF16)
    for d in order:
        for which in range(2):
            swap(which, d).wait_send()
        if d:
            cross(d).wait_send()


def body(x, g, w, r, ld, head_count):
    tokens, width = x.shape
    heads = ld.shape[0]
    state = w.shape[1]
    tiles = tokens // TILE
    limit = 60 * 1024 * 1024
    shape = jax.ShapeDtypeStruct
    vmem = pl.BlockSpec(memory_space=pltpu.VMEM)
    tile_rows = pl.BlockSpec((TILE, width), lambda k: (k, 0))
    tile_proj = pl.BlockSpec((TILE, state), lambda k: (k, 0))
    states, decay = pl.pallas_call(
        functools.partial(summary_kernel, heads),
        grid=(tiles,),
        in_specs=[tile_rows, tile_rows, tile_proj, tile_proj,
                  pl.BlockSpec((heads, TILE), lambda k: (0, k))],
        out_specs=[pl.BlockSpec((2, state, width), lambda k: (0, 0, 0)),
                   pl.BlockSpec((8, width), lambda k: (0, 0))],
        out_shape=[shape((2, state, width), F32), shape((8, width), F32)],
        scratch_shapes=[pltpu.VMEM((2 * heads, width), BF16)],
        compiler_params=pltpu.CompilerParams(vmem_limit_bytes=limit),
        name="summary",
    )(x, g, w, r, ld)
    chunks = state // CHUNK
    sem = pltpu.SemaphoreType.DMA
    buffer = pltpu.VMEM((state, width), F32)
    arriving = pl.pallas_call(
        chain_kernel,
        in_specs=[vmem, vmem],
        out_specs=vmem,
        out_shape=shape((2, state, width), F32),
        scratch_shapes=[buffer, buffer, buffer, buffer, pltpu.VMEM((8, width), F32)]
        + [sem((chunks,))] * 6 + [sem, sem],
        compiler_params=pltpu.CompilerParams(
            collective_id=0, has_side_effects=True, vmem_limit_bytes=limit),
        name="chain",
    )(states, decay)

    def early(i):
        return (jnp.minimum(i, tiles - 1), 0)

    def late(i):
        return (jnp.minimum(2 * tiles - 1 - i, tiles - 1), 0)

    whole2 = lambda i: (0, 0)
    grad_input, part_write, part_read = pl.pallas_call(
        functools.partial(main_kernel, heads, tiles),
        grid=(2 * tiles,),
        in_specs=[pl.BlockSpec((TILE, width), early), pl.BlockSpec((TILE, width), early),
                  pl.BlockSpec((tokens, state), whole2), pl.BlockSpec((tokens, state), whole2),
                  pl.BlockSpec((heads, tokens), whole2),
                  pl.BlockSpec((2, state, width), lambda i: (0, 0, 0))],
        out_specs=[pl.BlockSpec((TILE, width), late),
                   pl.BlockSpec((tokens, state), whole2), pl.BlockSpec((tokens, state), whole2)],
        out_shape=[shape((tokens, width), BF16), shape((tokens, state), F32),
                   shape((tokens, state), F32)],
        scratch_shapes=[pltpu.VMEM((2 * heads, width), BF16), pltpu.VMEM((tokens, width), BF16),
                        pltpu.VMEM((tokens, width), BF16), pltpu.VMEM((state, width), F32)],
        compiler_params=pltpu.CompilerParams(vmem_limit_bytes=limit),
        name="main",
    )(x, g, w, r, ld, arriving)
    size = tokens // head_count
    chips = head_count // 2
    grad_write, grad_read = pl.pallas_call(
        scatter_kernel,
        in_specs=[vmem, vmem],
        out_specs=[vmem, vmem],
        out_shape=[shape((size, state), BF16)] * 2,
        scratch_shapes=[pltpu.VMEM((2, chips, size, state), F32)] * 3
        + [sem((2, chips)), sem((2, chips)), sem((chips,)), sem((chips,))],
        compiler_params=pltpu.CompilerParams(
            collective_id=1, has_side_effects=True, vmem_limit_bytes=limit),
        name="scatter",
    )(part_write, part_read)
    return grad_input, grad_write, grad_read


def solution(mesh):
    return jax.shard_map(
        functools.partial(body, head_count=mesh.shape["head"]),
        mesh=mesh,
        in_specs=(
            P("seq", "head"),
            P("seq", "head"),
            P("seq", None),
            P("seq", None),
            P("head", "seq"),
        ),
        out_specs=(P("seq", "head"), P(("seq", "head"), None), P(("seq", "head"), None)),
        check_vma=False,
    )
```

```python
import functools
import jax
import jax.numpy as jnp
from jax import lax
from jax.experimental import pallas as pl
from jax.experimental.pallas import tpu as pltpu
from jax.sharding import PartitionSpec as P

TILE = 128
MID = TILE // 2 - 1
LANES = 256
MESH = pl.DeviceIdType.MESH
F32 = jnp.float32
BF16 = jnp.bfloat16


def dot(a, b, ca, cb):
    return lax.dot_general(a, b, (((ca,), (cb,)), ((), ())), preferred_element_type=F32)


def pieces(value, count, axis):
    parts = []
    for _ in range(count):
        part = value.astype(BF16)
        parts.append(part)
        value = value - part.astype(F32)
    return jnp.concatenate(parts, axis=axis)


def fill_expand(expand_ref, heads):
    groups, rows, lanes = expand_ref.shape
    size = groups * lanes // heads
    row = lax.broadcasted_iota(jnp.int32, (rows, lanes), 0)
    col = lax.broadcasted_iota(jnp.int32, (rows, lanes), 1)
    for c in range(groups):
        low = (row % heads) * size - c * lanes
        expand_ref[c] = jnp.where((col >= low) & (col < low + size), 1.0, 0.0).astype(BF16)


def fill_decays(ld_ref, up_ref, down_ref, ends_ref):
    tokens = ld_ref.shape[1]
    tiles = tokens // TILE
    row = lax.broadcasted_iota(jnp.int32, (TILE, TILE), 0)
    col = lax.broadcasted_iota(jnp.int32, (TILE, TILE), 1)
    rel = jnp.where(col <= row, 1.0, 0.0) - jnp.where(col <= MID, 1.0, 0.0)
    rel = jnp.concatenate([rel.astype(BF16)] * 3, 1)
    for k in range(tiles):
        span = slice(k * TILE, (k + 1) * TILE)
        value = dot(rel, pieces(ld_ref[:, span], 3, 1), 1, 1)
        up_ref[span] = pieces(jnp.exp(-value), 2, 1)
        down_ref[span] = pieces(jnp.exp(value), 2, 1)
    logs = pieces(ld_ref[...], 3, 1)
    tile = lax.broadcasted_iota(jnp.int32, (tiles, tokens), 0)
    token = lax.broadcasted_iota(jnp.int32, (tiles, tokens), 1)
    low, mid, high = tile * TILE, tile * TILE + MID, (tile + 1) * TILE
    sets = [
        (token >= low) & (token <= mid),
        (token > mid) & (token < high),
        (token >= low) & (token < high),
        token <= mid,
        token > mid,
        token >= 0,
    ]
    for n, chosen in enumerate(sets):
        marks = jnp.where(chosen, 1.0, 0.0).astype(BF16)
        value = dot(jnp.concatenate([marks] * 3, 1), logs, 1, 1)
        ends_ref[n * tiles:(n + 1) * tiles] = pieces(jnp.exp(value), 2, 1)


def layer_kernel(heads, groups, x_ref, g_ref, w_ref, r_ref, ld_ref, gi_ref, gw_ref, gr_ref,
                 expand_ref, up_ref, down_ref, ends_ref, rows_ref, left_ref, xs_ref, gs_ref,
                 sp_ref, gp_ref, loc_ref, got, prior, passed, theirs, val_ref, raw_ref, stage,
                 sa, ra, sb, rb, sc, rc, so):
    i = pl.program_id(0)
    me = lax.axis_index("seq")
    count = lax.axis_size("seq")
    tokens, lanes = x_ref.shape
    state = w_ref.shape[1]
    tiles = tokens // TILE
    odd = lax.rem(me, 2)
    partner = me + 1 - 2 * odd
    step = 4 * odd - 2
    nxt, prv, fed = me + step, me - step, partner + step
    has_next = (nxt >= 0) & (nxt < count)
    has_prev = (prv >= 0) & (prv < count)
    partner_prev = (fed >= 0) & (fed < count)
    mine, other = 1 - odd, odd
    c = lax.rem(i, groups)
    phase = i // groups

    def span(k):
        return slice(k * TILE, (k + 1) * TILE)

    def swap(c):
        return pltpu.make_async_remote_copy(
            loc_ref.at[c, other], got.at[c], sa.at[c], ra.at[c],
            device_id={"seq": partner}, device_id_type=MESH)

    def forward(c):
        return pltpu.make_async_remote_copy(
            passed.at[c], prior.at[c], sb.at[c], rb.at[c],
            device_id={"seq": nxt}, device_id_type=MESH)

    def hand(c):
        return pltpu.make_async_remote_copy(
            prior.at[c], theirs.at[c], sc.at[c], rc.at[c],
            device_id={"seq": partner}, device_id_type=MESH)

    def put(c):
        at = pl.ds(pl.multiple_of(c * lanes, lanes), lanes)
        return pltpu.make_async_copy(stage.at[c], gi_ref.at[:, at], so.at[c])

    @pl.when(i == 0)
    def _():
        barrier = pltpu.get_barrier_semaphore()
        pl.semaphore_signal(barrier, 1, device_id={"seq": partner}, device_id_type=MESH)

        @pl.when(has_next)
        def _():
            pl.semaphore_signal(barrier, 1, device_id={"seq": nxt}, device_id_type=MESH)

        @pl.when(has_prev)
        def _():
            pl.semaphore_signal(barrier, 1, device_id={"seq": prv}, device_id_type=MESH)

        fill_expand(expand_ref, heads)
        fill_decays(ld_ref, up_ref, down_ref, ends_ref)
        peers = 1 + has_next.astype(jnp.int32) + has_prev.astype(jnp.int32)
        pl.semaphore_wait(barrier, peers)

    @pl.when(phase == 0)
    def _():
        expand = expand_ref[c]
        rows = dot(ends_ref[...], expand, 1, 0)
        rows_ref[c] = rows
        xs = (x_ref[...].astype(F32) * dot(up_ref[...], expand, 1, 0)).astype(BF16)
        gs = (g_ref[...].astype(F32) * dot(down_ref[...], expand, 1, 0)).astype(BF16)
        xs_ref[c] = xs
        gs_ref[c] = gs
        carry = jnp.zeros((state, lanes), F32)
        for k in range(tiles):
            start, end, whole = (rows[n * tiles + k:n * tiles + k + 1] for n in range(3))
            sp_ref[c, k] = start * carry
            carry = whole * carry + end * dot(w_ref[span(k)], xs[span(k)], 0, 0)
        loc_ref[c, 0, :state] = carry
        carry = jnp.zeros((state, lanes), F32)
        for k in reversed(range(tiles)):
            start, end, whole = (rows[n * tiles + k:n * tiles + k + 1] for n in range(3))
            gp_ref[c, k] = end * carry
            carry = whole * carry + start * dot(r_ref[span(k)], gs[span(k)], 0, 0)
        loc_ref[c, 1, :state] = carry
        decay = jnp.broadcast_to(rows[5 * tiles:5 * tiles + 1], (8, lanes))
        loc_ref[c, 0, state:] = decay
        loc_ref[c, 1, state:] = decay
        swap(c).start()

    @pl.when(i == groups - 1)
    def _():
        row = lax.broadcasted_iota(jnp.int32, (TILE, TILE), 0)
        col = lax.broadcasted_iota(jnp.int32, (TILE, TILE), 1)
        for k in range(tiles):
            pairs = jnp.where(col >= row, dot(w_ref[span(k)], r_ref[span(k)], 1, 1), 0.0)
            left_ref[span(k), :TILE] = pairs.astype(BF16)
            left_ref[span(k), TILE:] = w_ref[span(k)]
        gw_ref[...] = jnp.zeros_like(gw_ref)
        gr_ref[...] = jnp.zeros_like(gr_ref)
        raw_ref[...] = jnp.zeros_like(raw_ref)

    @pl.when(phase == 1)
    def _():
        swap(c).wait_recv()
        own = rows_ref[c, 5 * tiles:5 * tiles + 1]
        partners = got[c, state:state + 1]
        summed = own * got[c, :state] + loc_ref[c, mine, :state]

        @pl.when(has_prev)
        def _():
            forward(c).wait_recv()
            hand(c).start()
            passed[c] = (own * partners) * prior[c] + summed
            val_ref[...] = partners * prior[c] + got[c, :state]

        @pl.when(jnp.logical_not(has_prev))
        def _():
            passed[c] = summed
            val_ref[...] = got[c, :state]

        @pl.when(has_next)
        def _():
            forward(c).start()

        for k in range(tiles):
            raw_ref[span(k)] += dot(xs_ref[c, span(k)], gs_ref[c, span(k)], 1, 1)

    @pl.when(phase == 2)
    def _():
        @pl.when(partner_prev)
        def _():
            hand(c).wait_recv()
            val_ref[...] = theirs[c]

        @pl.when(jnp.logical_not(partner_prev))
        def _():
            val_ref[...] = jnp.zeros_like(val_ref)

    @pl.when(phase == 2 - odd)
    def _():
        value = val_ref[...]
        for k in range(tiles):
            scale = rows_ref[c, 3 * tiles + k:3 * tiles + k + 1]
            entering = (sp_ref[c, k] + scale * value).astype(BF16)
            gr_ref[span(k)] += dot(gs_ref[c, span(k)], entering, 1, 1)

    @pl.when(phase == 1 + odd)
    def _():
        value = val_ref[...]
        expand = expand_ref[c]
        for k in range(tiles):
            scale = rows_ref[c, 4 * tiles + k:4 * tiles + k + 1]
            leaving = (gp_ref[c, k] + scale * value).astype(BF16)
            right = jnp.concatenate([gs_ref[c, span(k)], leaving], 0)
            up = dot(up_ref[span(k)], expand, 1, 0)
            stage[c, span(k)] = (up * dot(left_ref[span(k)], right, 1, 0)).astype(BF16)
            gw_ref[span(k)] += dot(xs_ref[c, span(k)], leaving, 1, 1)
        put(c).start()

    @pl.when(i == 2 * groups)
    def _():
        row = lax.broadcasted_iota(jnp.int32, (TILE, TILE), 0)
        col = lax.broadcasted_iota(jnp.int32, (TILE, TILE), 1)
        for k in range(tiles):
            weights = jnp.where(col >= row, raw_ref[span(k)], 0.0).astype(BF16)
            gw_ref[span(k)] += dot(weights, r_ref[span(k)], 1, 0)
            gr_ref[span(k)] += dot(weights, w_ref[span(k)], 0, 0)

    @pl.when(i == 3 * groups - 1)
    def _():
        for n in range(groups):
            put(n).wait()
            swap(n).wait_send()

            @pl.when(has_prev)
            def _():
                hand(n).wait_send()

            @pl.when(has_next)
            def _():
                forward(n).wait_send()


def scatter_kernel(gw_ref, gr_ref, ow_ref, or_ref, near, half, far, sa, ra, sb, rb):
    me = lax.axis_index("head")
    count = lax.axis_size("head")
    chips = count // 2
    core = lax.rem(me, 2)
    chip = me // 2
    mate = me + 1 - 2 * core
    size = ow_ref.shape[0]
    barrier = pltpu.get_barrier_semaphore()
    pl.semaphore_signal(barrier, 1, device_id={"head": mate}, device_id_type=MESH)
    for d in range(1, chips):
        there = 2 * lax.rem(chip + d, chips) + core
        pl.semaphore_signal(barrier, 1, device_id={"head": there}, device_id_type=MESH)
    pl.semaphore_wait(barrier, chips)

    def block(h):
        return pl.ds(pl.multiple_of(h * size, size), size)

    def swap(which, d):
        at = 2 * lax.rem(chip + d, chips) + 1 - core
        ref = (gw_ref, gr_ref)[which]
        return pltpu.make_async_remote_copy(
            ref.at[block(at)], near.at[which, d], sa.at[which, d], ra.at[which, d],
            device_id={"head": mate}, device_id_type=MESH)

    def cross(d):
        there = 2 * lax.rem(chip + d, chips) + core
        return pltpu.make_async_remote_copy(
            half.at[:, d], far.at[:, d], sb.at[d], rb.at[d],
            device_id={"head": there}, device_id_type=MESH)

    order = [d for d in range(1, chips)] + [0]
    for d in order:
        for which in range(2):
            swap(which, d).start()
    for d in order:
        at = 2 * lax.rem(chip + d, chips) + core
        for which, ref in enumerate((gw_ref, gr_ref)):
            swap(which, d).wait_recv()
            half[which, d] = near[which, d] + ref[block(at)]
        if d:
            cross(d).start()
    total = [half[0, 0], half[1, 0]]
    for d in range(1, chips):
        cross(d).wait_recv()
        total = [total[0] + far[0, d], total[1] + far[1, d]]
    ow_ref[...] = total[0].astype(BF16)
    or_ref[...] = total[1].astype(BF16)
    for d in order:
        for which in range(2):
            swap(which, d).wait_send()
        if d:
            cross(d).wait_send()


def body(x, g, w, r, ld, head_count):
    tokens, width = x.shape
    heads = ld.shape[0]
    state = w.shape[1]
    tiles = tokens // TILE
    limit = 60 * 1024 * 1024
    shape = jax.ShapeDtypeStruct
    vmem = pl.BlockSpec(memory_space=pltpu.VMEM)
    sem = pltpu.SemaphoreType.DMA
    lanes = min(LANES, width)
    groups = width // lanes
    whole = lambda i: (0, 0)
    columns = pl.BlockSpec((tokens, lanes), lambda i: (0, jnp.minimum(i, groups - 1)))
    slabs = pltpu.VMEM((groups, state, lanes), F32)
    tall = pltpu.VMEM((groups, state + 8, lanes), F32)
    grad_input, part_write, part_read = pl.pallas_call(
        functools.partial(layer_kernel, heads, groups),
        grid=(3 * groups,),
        in_specs=[columns, columns,
                  pl.BlockSpec((tokens, state), whole), pl.BlockSpec((tokens, state), whole),
                  pl.BlockSpec((heads, tokens), whole)],
        out_specs=[pl.BlockSpec(memory_space=pl.ANY),
                   pl.BlockSpec((tokens, state), whole), pl.BlockSpec((tokens, state), whole)],
        out_shape=[shape((tokens, width), BF16), shape((tokens, state), F32),
                   shape((tokens, state), F32)],
        scratch_shapes=[
            pltpu.VMEM((groups, 2 * heads, lanes), BF16),
            pltpu.VMEM((tokens, 2 * heads), BF16),
            pltpu.VMEM((tokens, 2 * heads), BF16),
            pltpu.VMEM((6 * tiles, 2 * heads), BF16),
            pltpu.VMEM((groups, 6 * tiles, lanes), F32),
            pltpu.VMEM((tokens, TILE + state), BF16),
            pltpu.VMEM((groups, tokens, lanes), BF16),
            pltpu.VMEM((groups, tokens, lanes), BF16),
            pltpu.VMEM((groups, tiles, state, lanes), F32),
            pltpu.VMEM((groups, tiles, state, lanes), F32),
            pltpu.VMEM((groups, 2, state + 8, lanes), F32),
            tall, slabs, slabs, slabs,
            pltpu.VMEM((state, lanes), F32),
            pltpu.VMEM((tokens, TILE), F32),
            pltpu.VMEM((groups, tokens, lanes), BF16),
        ] + [sem((groups,))] * 7,
        compiler_params=pltpu.CompilerParams(
            collective_id=0, has_side_effects=True, vmem_limit_bytes=limit),
        name="layer",
    )(x, g, w, r, ld)
    size = tokens // head_count
    chips = head_count // 2
    grad_write, grad_read = pl.pallas_call(
        scatter_kernel,
        in_specs=[vmem, vmem],
        out_specs=[vmem, vmem],
        out_shape=[shape((size, state), BF16)] * 2,
        scratch_shapes=[pltpu.VMEM((2, chips, size, state), F32)] * 3
        + [sem((2, chips)), sem((2, chips)), sem((chips,)), sem((chips,))],
        compiler_params=pltpu.CompilerParams(
            collective_id=1, has_side_effects=True, vmem_limit_bytes=limit),
        name="scatter",
    )(part_write, part_read)
    return grad_input, grad_write, grad_read


def solution(mesh):
    return jax.shard_map(
        functools.partial(body, head_count=mesh.shape["head"]),
        mesh=mesh,
        in_specs=(
            P("seq", "head"),
            P("seq", "head"),
            P("seq", None),
            P("seq", None),
            P("head", "seq"),
        ),
        out_specs=(P("seq", "head"), P(("seq", "head"), None), P(("seq", "head"), None)),
        check_vma=False,
    )
```

```python
import functools
import jax
import jax.numpy as jnp
from jax import lax
from jax.experimental import pallas as pl
from jax.experimental.pallas import tpu as pltpu
from jax.sharding import PartitionSpec as P

TILE = 128
MID = TILE // 2 - 1
LANES = 256
MESH = pl.DeviceIdType.MESH
F32 = jnp.float32
BF16 = jnp.bfloat16


def dot(a, b, ca, cb):
    return lax.dot_general(a, b, (((ca,), (cb,)), ((), ())), preferred_element_type=F32)


def pieces(value, count, axis):
    parts = []
    for _ in range(count):
        part = value.astype(BF16)
        parts.append(part)
        value = value - part.astype(F32)
    return jnp.concatenate(parts, axis=axis)


def fill_expand(expand_ref, heads):
    groups, rows, lanes = expand_ref.shape
    size = groups * lanes // heads
    row = lax.broadcasted_iota(jnp.int32, (rows, lanes), 0)
    col = lax.broadcasted_iota(jnp.int32, (rows, lanes), 1)
    for c in range(groups):
        low = (row % heads) * size - c * lanes
        expand_ref[c] = jnp.where((col >= low) & (col < low + size), 1.0, 0.0).astype(BF16)


def fill_decays(ld_ref, up_ref, down_ref, ends_ref):
    tokens = ld_ref.shape[1]
    tiles = tokens // TILE
    row = lax.broadcasted_iota(jnp.int32, (TILE, TILE), 0)
    col = lax.broadcasted_iota(jnp.int32, (TILE, TILE), 1)
    rel = jnp.where(col <= row, 1.0, 0.0) - jnp.where(col <= MID, 1.0, 0.0)
    rel = jnp.concatenate([rel.astype(BF16)] * 3, 1)
    for k in range(tiles):
        span = slice(k * TILE, (k + 1) * TILE)
        value = dot(rel, pieces(ld_ref[:, span], 3, 1), 1, 1)
        up_ref[span] = pieces(jnp.exp(-value), 2, 1)
        down_ref[span] = pieces(jnp.exp(value), 2, 1)
    logs = pieces(ld_ref[...], 3, 1)
    tile = lax.broadcasted_iota(jnp.int32, (tiles, tokens), 0)
    token = lax.broadcasted_iota(jnp.int32, (tiles, tokens), 1)
    low, mid, high = tile * TILE, tile * TILE + MID, (tile + 1) * TILE
    sets = [
        (token >= low) & (token <= mid),
        (token > mid) & (token < high),
        (token >= low) & (token < high),
        token <= mid,
        token > mid,
        token >= 0,
    ]
    for n, chosen in enumerate(sets):
        marks = jnp.where(chosen, 1.0, 0.0).astype(BF16)
        value = dot(jnp.concatenate([marks] * 3, 1), logs, 1, 1)
        ends_ref[n * tiles:(n + 1) * tiles] = pieces(jnp.exp(value), 2, 1)


def layer_kernel(heads, groups, x_ref, g_ref, w_ref, r_ref, ld_ref, gi_ref, early_ref, late_ref,
                 expand_ref, up_ref, down_ref, ends_ref, rows_ref, left_ref, xs_ref, gs_ref,
                 sp_ref, gp_ref, loc_ref, got, prior, passed, theirs, val_ref, raw_ref, stage,
                 acc_ref, near, half, far, sa, ra, sb, rb, sc, rc, so, sn, rn, sf, rf):
    i = pl.program_id(0)
    me = lax.axis_index("seq")
    count = lax.axis_size("seq")
    tokens, lanes = x_ref.shape
    state = w_ref.shape[1]
    tiles = tokens // TILE
    odd = lax.rem(me, 2)
    partner = me + 1 - 2 * odd
    step = 4 * odd - 2
    nxt, prv, fed = me + step, me - step, partner + step
    has_next = (nxt >= 0) & (nxt < count)
    has_prev = (prv >= 0) & (prv < count)
    partner_prev = (fed >= 0) & (fed < count)
    mine, other = 1 - odd, odd
    gw, gr = odd, 1 - odd
    ring = Ring(acc_ref.at[0], near, half, far, sn, rn, sf, rf)
    c = lax.rem(i, groups)
    phase = i // groups

    def span(k):
        return slice(k * TILE, (k + 1) * TILE)

    def swap(c):
        return pltpu.make_async_remote_copy(
            loc_ref.at[c, other], got.at[c], sa.at[c], ra.at[c],
            device_id={"seq": partner}, device_id_type=MESH)

    def forward(c):
        return pltpu.make_async_remote_copy(
            passed.at[c], prior.at[c], sb.at[c], rb.at[c],
            device_id={"seq": nxt}, device_id_type=MESH)

    def hand(c):
        return pltpu.make_async_remote_copy(
            prior.at[c], theirs.at[c], sc.at[c], rc.at[c],
            device_id={"seq": partner}, device_id_type=MESH)

    def put(c):
        at = pl.ds(pl.multiple_of(c * lanes, lanes), lanes)
        return pltpu.make_async_copy(stage.at[c], gi_ref.at[:, at], so.at[c])

    @pl.when(i == 0)
    def _():
        barrier = pltpu.get_barrier_semaphore()
        pl.semaphore_signal(barrier, 1, device_id={"seq": partner}, device_id_type=MESH)

        @pl.when(has_next)
        def _():
            pl.semaphore_signal(barrier, 1, device_id={"seq": nxt}, device_id_type=MESH)

        @pl.when(has_prev)
        def _():
            pl.semaphore_signal(barrier, 1, device_id={"seq": prv}, device_id_type=MESH)

        fill_expand(expand_ref, heads)
        fill_decays(ld_ref, up_ref, down_ref, ends_ref)
        ring.greet(barrier)
        peers = ring.chips + 1 + has_next.astype(jnp.int32) + has_prev.astype(jnp.int32)
        pl.semaphore_wait(barrier, peers)

    @pl.when(phase == 0)
    def _():
        expand = expand_ref[c]
        rows = dot(ends_ref[...], expand, 1, 0)
        rows_ref[c] = rows
        xs = (x_ref[...].astype(F32) * dot(up_ref[...], expand, 1, 0)).astype(BF16)
        gs = (g_ref[...].astype(F32) * dot(down_ref[...], expand, 1, 0)).astype(BF16)
        xs_ref[c] = xs
        gs_ref[c] = gs
        carry = jnp.zeros((state, lanes), F32)
        for k in range(tiles):
            start, end, whole = (rows[n * tiles + k:n * tiles + k + 1] for n in range(3))
            sp_ref[c, k] = start * carry
            carry = whole * carry + end * dot(w_ref[span(k)], xs[span(k)], 0, 0)
        loc_ref[c, 0, :state] = carry
        carry = jnp.zeros((state, lanes), F32)
        for k in reversed(range(tiles)):
            start, end, whole = (rows[n * tiles + k:n * tiles + k + 1] for n in range(3))
            gp_ref[c, k] = end * carry
            carry = whole * carry + start * dot(r_ref[span(k)], gs[span(k)], 0, 0)
        loc_ref[c, 1, :state] = carry
        decay = jnp.broadcast_to(rows[5 * tiles:5 * tiles + 1], (8, lanes))
        loc_ref[c, 0, state:] = decay
        loc_ref[c, 1, state:] = decay
        swap(c).start()

    @pl.when(i == groups - 1)
    def _():
        row = lax.broadcasted_iota(jnp.int32, (TILE, TILE), 0)
        col = lax.broadcasted_iota(jnp.int32, (TILE, TILE), 1)
        for k in range(tiles):
            pairs = jnp.where(col >= row, dot(w_ref[span(k)], r_ref[span(k)], 1, 1), 0.0)
            left_ref[span(k), :TILE] = pairs.astype(BF16)
            left_ref[span(k), TILE:] = w_ref[span(k)]
        acc_ref[...] = jnp.zeros_like(acc_ref)
        raw_ref[...] = jnp.zeros_like(raw_ref)

    @pl.when(phase == 1)
    def _():
        swap(c).wait_recv()
        own = rows_ref[c, 5 * tiles:5 * tiles + 1]
        partners = got[c, state:state + 1]
        summed = own * got[c, :state] + loc_ref[c, mine, :state]

        @pl.when(has_prev)
        def _():
            forward(c).wait_recv()
            hand(c).start()
            passed[c] = (own * partners) * prior[c] + summed
            val_ref[...] = partners * prior[c] + got[c, :state]

        @pl.when(jnp.logical_not(has_prev))
        def _():
            passed[c] = summed
            val_ref[...] = got[c, :state]

        @pl.when(has_next)
        def _():
            forward(c).start()

        for k in range(tiles):
            raw_ref[span(k)] += dot(xs_ref[c, span(k)], gs_ref[c, span(k)], 1, 1)

    @pl.when(phase == 2)
    def _():
        @pl.when(partner_prev)
        def _():
            hand(c).wait_recv()
            val_ref[...] = theirs[c]

        @pl.when(jnp.logical_not(partner_prev))
        def _():
            val_ref[...] = jnp.zeros_like(val_ref)

    @pl.when(phase == 2 - odd)
    def _():
        value = val_ref[...]
        for k in range(tiles):
            scale = rows_ref[c, 3 * tiles + k:3 * tiles + k + 1]
            entering = (sp_ref[c, k] + scale * value).astype(BF16)
            acc_ref[gr, span(k)] += dot(gs_ref[c, span(k)], entering, 1, 1)

    @pl.when(phase == 1 + odd)
    def _():
        value = val_ref[...]
        expand = expand_ref[c]
        for k in range(tiles):
            scale = rows_ref[c, 4 * tiles + k:4 * tiles + k + 1]
            leaving = (gp_ref[c, k] + scale * value).astype(BF16)
            right = jnp.concatenate([gs_ref[c, span(k)], leaving], 0)
            up = dot(up_ref[span(k)], expand, 1, 0)
            stage[c, span(k)] = (up * dot(left_ref[span(k)], right, 1, 0)).astype(BF16)
            acc_ref[gw, span(k)] += dot(xs_ref[c, span(k)], leaving, 1, 1)
        put(c).start()

    @pl.when(i == 2 * groups)
    def _():
        row = lax.broadcasted_iota(jnp.int32, (TILE, TILE), 0)
        col = lax.broadcasted_iota(jnp.int32, (TILE, TILE), 1)
        for k in range(tiles):
            weights = jnp.where(col >= row, raw_ref[span(k)], 0.0).astype(BF16)
            acc_ref[gw, span(k)] += dot(weights, r_ref[span(k)], 1, 0)
            acc_ref[gr, span(k)] += dot(weights, w_ref[span(k)], 0, 0)
        ring.start()

    @pl.when(i == 2 * groups + 1)
    def _():
        ring.join()

    @pl.when(i == 2 * groups + 3)
    def _():
        early_ref[...] = ring.total()

    @pl.when(i == 3 * groups - 1)
    def _():
        late_ref[...] = acc_ref[1]
        ring.drain()
        for n in range(groups):
            put(n).wait()
            swap(n).wait_send()

            @pl.when(has_prev)
            def _():
                hand(n).wait_send()

            @pl.when(has_next)
            def _():
                forward(n).wait_send()


class Ring:
    def __init__(self, source, near, half, far, sa, ra, sb, rb):
        self.me = lax.axis_index("head")
        self.chips = lax.axis_size("head") // 2
        self.core = lax.rem(self.me, 2)
        self.chip = self.me // 2
        self.mate = self.me + 1 - 2 * self.core
        self.order = list(range(1, self.chips)) + [0]
        self.size = near.shape[1]
        self.source, self.near, self.half, self.far = source, near, half, far
        self.sems = sa, ra, sb, rb

    def peer(self, d):
        return 2 * lax.rem(self.chip + d, self.chips) + self.core

    def greet(self, barrier):
        pl.semaphore_signal(barrier, 1, device_id={"head": self.mate}, device_id_type=MESH)
        for d in range(1, self.chips):
            pl.semaphore_signal(barrier, 1, device_id={"head": self.peer(d)}, device_id_type=MESH)

    def block(self, h):
        return pl.ds(pl.multiple_of(h * self.size, self.size), self.size)

    def swap(self, d):
        sa, ra, _, _ = self.sems
        at = self.peer(d) + 1 - 2 * self.core
        return pltpu.make_async_remote_copy(
            self.source.at[self.block(at)], self.near.at[d], sa.at[d], ra.at[d],
            device_id={"head": self.mate}, device_id_type=MESH)

    def cross(self, d):
        _, _, sb, rb = self.sems
        return pltpu.make_async_remote_copy(
            self.half.at[d], self.far.at[d], sb.at[d], rb.at[d],
            device_id={"head": self.peer(d)}, device_id_type=MESH)

    def start(self):
        for d in self.order:
            self.swap(d).start()

    def join(self):
        for d in self.order:
            self.swap(d).wait_recv()
            self.half[d] = self.near[d] + self.source[self.block(self.peer(d))]
            if d:
                self.cross(d).start()

    def total(self):
        total = self.half[0]
        for d in range(1, self.chips):
            self.cross(d).wait_recv()
            total = total + self.far[d]
        return total.astype(BF16)

    def drain(self):
        for d in self.order:
            self.swap(d).wait_send()
            if d:
                self.cross(d).wait_send()


def scatter_kernel(early_ref, late_ref, ow_ref, or_ref, near, half, far, sa, ra, sb, rb):
    ring = Ring(late_ref, near, half, far, sa, ra, sb, rb)
    odd = lax.rem(lax.axis_index("seq"), 2)
    barrier = pltpu.get_barrier_semaphore()
    ring.greet(barrier)
    pl.semaphore_wait(barrier, ring.chips)
    ring.start()
    ring.join()
    late = ring.total()

    @pl.when(odd == 1)
    def _():
        or_ref[...] = early_ref[...]
        ow_ref[...] = late

    @pl.when(odd == 0)
    def _():
        ow_ref[...] = early_ref[...]
        or_ref[...] = late

    ring.drain()


def body(x, g, w, r, ld, head_count):
    tokens, width = x.shape
    heads = ld.shape[0]
    state = w.shape[1]
    tiles = tokens // TILE
    limit = 60 * 1024 * 1024
    shape = jax.ShapeDtypeStruct
    vmem = pl.BlockSpec(memory_space=pltpu.VMEM)
    sem = pltpu.SemaphoreType.DMA
    lanes = min(LANES, width)
    groups = width // lanes
    whole = lambda i: (0, 0)
    columns = pl.BlockSpec((tokens, lanes), lambda i: (0, jnp.minimum(i, groups - 1)))
    slabs = pltpu.VMEM((groups, state, lanes), F32)
    tall = pltpu.VMEM((groups, state + 8, lanes), F32)
    size = tokens // head_count
    chips = head_count // 2
    links = [pltpu.VMEM((chips, size, state), F32)] * 3
    grad_input, early, late = pl.pallas_call(
        functools.partial(layer_kernel, heads, groups),
        grid=(3 * groups,),
        in_specs=[columns, columns,
                  pl.BlockSpec((tokens, state), whole), pl.BlockSpec((tokens, state), whole),
                  pl.BlockSpec((heads, tokens), whole)],
        out_specs=[pl.BlockSpec(memory_space=pl.ANY),
                   pl.BlockSpec((size, state), whole), pl.BlockSpec((tokens, state), whole)],
        out_shape=[shape((tokens, width), BF16), shape((size, state), BF16),
                   shape((tokens, state), F32)],
        scratch_shapes=[
            pltpu.VMEM((groups, 2 * heads, lanes), BF16),
            pltpu.VMEM((tokens, 2 * heads), BF16),
            pltpu.VMEM((tokens, 2 * heads), BF16),
            pltpu.VMEM((6 * tiles, 2 * heads), BF16),
            pltpu.VMEM((groups, 6 * tiles, lanes), F32),
            pltpu.VMEM((tokens, TILE + state), BF16),
            pltpu.VMEM((groups, tokens, lanes), BF16),
            pltpu.VMEM((groups, tokens, lanes), BF16),
            pltpu.VMEM((groups, tiles, state, lanes), F32),
            pltpu.VMEM((groups, tiles, state, lanes), F32),
            pltpu.VMEM((groups, 2, state + 8, lanes), F32),
            tall, slabs, slabs, slabs,
            pltpu.VMEM((state, lanes), F32),
            pltpu.VMEM((tokens, TILE), F32),
            pltpu.VMEM((groups, tokens, lanes), BF16),
            pltpu.VMEM((2, tokens, state), F32),
        ] + links + [sem((groups,))] * 7 + [sem((chips,))] * 4,
        compiler_params=pltpu.CompilerParams(
            collective_id=0, has_side_effects=True, vmem_limit_bytes=limit),
        name="layer",
    )(x, g, w, r, ld)
    grad_write, grad_read = pl.pallas_call(
        scatter_kernel,
        in_specs=[vmem, vmem],
        out_specs=[vmem, vmem],
        out_shape=[shape((size, state), BF16)] * 2,
        scratch_shapes=links + [sem((chips,))] * 4,
        compiler_params=pltpu.CompilerParams(
            collective_id=1, has_side_effects=True, vmem_limit_bytes=8 * 1024 * 1024),
        name="scatter",
    )(early, late)
    return grad_input, grad_write, grad_read


def solution(mesh):
    return jax.shard_map(
        functools.partial(body, head_count=mesh.shape["head"]),
        mesh=mesh,
        in_specs=(
            P("seq", "head"),
            P("seq", "head"),
            P("seq", None),
            P("seq", None),
            P("head", "seq"),
        ),
        out_specs=(P("seq", "head"), P(("seq", "head"), None), P(("seq", "head"), None)),
        check_vma=False,
    )
```

```python
import functools
import jax
import jax.numpy as jnp
from jax import lax
from jax.experimental import pallas as pl
from jax.experimental.pallas import tpu as pltpu
from jax.sharding import PartitionSpec as P

TILE = 128
MID = TILE // 2 - 1
LANES = 256
MESH = pl.DeviceIdType.MESH
F32 = jnp.float32
BF16 = jnp.bfloat16


def dot(a, b, ca, cb):
    return lax.dot_general(a, b, (((ca,), (cb,)), ((), ())), preferred_element_type=F32)


def pieces(value, count, axis):
    parts = []
    for _ in range(count):
        part = value.astype(BF16)
        parts.append(part)
        value = value - part.astype(F32)
    return jnp.concatenate(parts, axis=axis)


def fill_expand(expand_ref, heads):
    groups, rows, lanes = expand_ref.shape
    size = groups * lanes // heads
    row = lax.broadcasted_iota(jnp.int32, (rows, lanes), 0)
    col = lax.broadcasted_iota(jnp.int32, (rows, lanes), 1)
    for c in range(groups):
        low = (row % heads) * size - c * lanes
        expand_ref[c] = jnp.where((col >= low) & (col < low + size), 1.0, 0.0).astype(BF16)


def fill_decays(ld_ref, up_ref, down_ref, ends_ref, dec_ref):
    tokens = ld_ref.shape[1]
    tiles = tokens // TILE
    row = lax.broadcasted_iota(jnp.int32, (TILE, TILE), 0)
    col = lax.broadcasted_iota(jnp.int32, (TILE, TILE), 1)
    rel = jnp.where(col <= row, 1.0, 0.0) - jnp.where(col <= MID, 1.0, 0.0)
    rel = jnp.concatenate([rel.astype(BF16)] * 3, 1)
    for k in range(tiles):
        span = slice(k * TILE, (k + 1) * TILE)
        value = dot(rel, pieces(ld_ref[:, span], 3, 1), 1, 1)
        up_ref[span] = pieces(jnp.exp(-value), 2, 1)
        down_ref[span] = pieces(jnp.exp(value), 2, 1)
    logs = pieces(ld_ref[...], 3, 1)
    tile = lax.broadcasted_iota(jnp.int32, (tiles, tokens), 0)
    token = lax.broadcasted_iota(jnp.int32, (tiles, tokens), 1)
    low, mid, high = tile * TILE, tile * TILE + MID, (tile + 1) * TILE
    sets = [
        (token >= low) & (token <= mid),
        (token > mid) & (token < high),
        (token >= low) & (token < high),
        token <= mid,
        token > mid,
        token >= 0,
    ]
    for n, chosen in enumerate(sets):
        marks = jnp.where(chosen, 1.0, 0.0).astype(BF16)
        value = dot(jnp.concatenate([marks] * 3, 1), logs, 1, 1)
        ends_ref[n * tiles:(n + 1) * tiles] = pieces(jnp.exp(value), 2, 1)
    dec_ref[...] = jnp.broadcast_to(jnp.exp(value)[:1], dec_ref.shape)


def layer_kernel(heads, groups, x_ref, g_ref, w_ref, r_ref, ld_ref, gi_ref, ow_ref, or_ref,
                 expand_ref, up_ref, down_ref, ends_ref, rows_ref, left_ref, xs_ref, gs_ref,
                 sp_ref, gp_ref, loc_ref, got, prior, passed, theirs, val_ref, raw_ref, dec_ref, gotdec,
                 acc_ref, near, half, far, near2, half2, far2, sa, ra, sb, rb, sc, rc, sd, rd,
                 sn, rn, sf, rf, sn2, rn2, sf2, rf2):
    i = pl.program_id(0)
    me = lax.axis_index("seq")
    count = lax.axis_size("seq")
    tokens, lanes = x_ref.shape
    state = w_ref.shape[1]
    tiles = tokens // TILE
    odd = lax.rem(me, 2)
    partner = me + 1 - 2 * odd
    step = 4 * odd - 2
    nxt, prv, fed = me + step, me - step, partner + step
    has_next = (nxt >= 0) & (nxt < count)
    has_prev = (prv >= 0) & (prv < count)
    partner_prev = (fed >= 0) & (fed < count)
    mine, other = 1 - odd, odd
    gw, gr = odd, 1 - odd
    ring = Ring(acc_ref.at[0], near, half, far, sn, rn, sf, rf)
    ring2 = Ring(acc_ref.at[1], near2, half2, far2, sn2, rn2, sf2, rf2)
    ratio = pltpu.make_async_remote_copy(
        dec_ref, gotdec, sd, rd, device_id={"seq": partner}, device_id_type=MESH)
    c = lax.rem(i, groups)
    phase = i // groups
    cols = pl.ds(pl.multiple_of(c * lanes, lanes), lanes)

    def span(k):
        return slice(k * TILE, (k + 1) * TILE)

    def swap(c):
        return pltpu.make_async_remote_copy(
            loc_ref.at[c, other], got.at[c], sa.at[c], ra.at[c],
            device_id={"seq": partner}, device_id_type=MESH)

    def forward(c):
        return pltpu.make_async_remote_copy(
            passed.at[c], prior.at[c], sb.at[c], rb.at[c],
            device_id={"seq": nxt}, device_id_type=MESH)

    def hand(c):
        return pltpu.make_async_remote_copy(
            prior.at[c], theirs.at[c], sc.at[c], rc.at[c],
            device_id={"seq": partner}, device_id_type=MESH)

    @pl.when(i == 0)
    def _():
        barrier = pltpu.get_barrier_semaphore()
        pl.semaphore_signal(barrier, 1, device_id={"seq": partner}, device_id_type=MESH)

        @pl.when(has_next)
        def _():
            pl.semaphore_signal(barrier, 1, device_id={"seq": nxt}, device_id_type=MESH)

        @pl.when(has_prev)
        def _():
            pl.semaphore_signal(barrier, 1, device_id={"seq": prv}, device_id_type=MESH)

        fill_expand(expand_ref, heads)
        fill_decays(ld_ref, up_ref, down_ref, ends_ref, dec_ref)
        ring.greet(barrier)
        peers = ring.chips + 1 + has_next.astype(jnp.int32) + has_prev.astype(jnp.int32)
        pl.semaphore_wait(barrier, peers)
        ratio.start()

    @pl.when(phase == 0)
    def _():
        expand = expand_ref[c]
        rows = dot(ends_ref[...], expand, 1, 0)
        rows_ref[c] = rows
        xs = (x_ref[...].astype(F32) * dot(up_ref[...], expand, 1, 0)).astype(BF16)
        gs = (g_ref[...].astype(F32) * dot(down_ref[...], expand, 1, 0)).astype(BF16)
        xs_ref[c] = xs
        gs_ref[c] = gs
        carry = jnp.zeros((state, lanes), F32)
        for k in range(tiles):
            start, end, whole = (rows[n * tiles + k:n * tiles + k + 1] for n in range(3))
            sp_ref[c, k] = start * carry
            carry = whole * carry + end * dot(w_ref[span(k)], xs[span(k)], 0, 0)
        loc_ref[c, 0] = carry
        carry = jnp.zeros((state, lanes), F32)
        for k in reversed(range(tiles)):
            start, end, whole = (rows[n * tiles + k:n * tiles + k + 1] for n in range(3))
            gp_ref[c, k] = end * carry
            carry = whole * carry + start * dot(r_ref[span(k)], gs[span(k)], 0, 0)
        loc_ref[c, 1] = carry
        swap(c).start()

    @pl.when(i == groups - 1)
    def _():
        ratio.wait_recv()
        row = lax.broadcasted_iota(jnp.int32, (TILE, TILE), 0)
        col = lax.broadcasted_iota(jnp.int32, (TILE, TILE), 1)
        for k in range(tiles):
            pairs = jnp.where(col >= row, dot(w_ref[span(k)], r_ref[span(k)], 1, 1), 0.0)
            left_ref[span(k), :TILE] = pairs.astype(BF16)
            left_ref[span(k), TILE:] = w_ref[span(k)]
        acc_ref[...] = jnp.zeros_like(acc_ref)
        raw_ref[...] = jnp.zeros_like(raw_ref)

    @pl.when(phase == 1)
    def _():
        swap(c).wait_recv()
        own = rows_ref[c, 5 * tiles:5 * tiles + 1]
        partners = dot(pieces(gotdec[...], 2, 1), expand_ref[c], 1, 0)[0:1]
        summed = own * got[c] + loc_ref[c, mine]

        @pl.when(has_prev)
        def _():
            forward(c).wait_recv()
            hand(c).start()
            passed[c] = (own * partners) * prior[c] + summed
            val_ref[...] = partners * prior[c] + got[c]

        @pl.when(jnp.logical_not(has_prev))
        def _():
            passed[c] = summed
            val_ref[...] = got[c]

        @pl.when(has_next)
        def _():
            forward(c).start()

        for k in range(tiles):
            raw_ref[span(k)] += dot(xs_ref[c, span(k)], gs_ref[c, span(k)], 1, 1)

    @pl.when(phase == 2)
    def _():
        @pl.when(partner_prev)
        def _():
            hand(c).wait_recv()
            val_ref[...] = theirs[c]

        @pl.when(jnp.logical_not(partner_prev))
        def _():
            val_ref[...] = jnp.zeros_like(val_ref)

    @pl.when(phase == 2 - odd)
    def _():
        value = val_ref[...]
        for k in range(tiles):
            scale = rows_ref[c, 3 * tiles + k:3 * tiles + k + 1]
            entering = (sp_ref[c, k] + scale * value).astype(BF16)
            acc_ref[gr, span(k)] += dot(gs_ref[c, span(k)], entering, 1, 1)

    @pl.when(phase == 1 + odd)
    def _():
        value = val_ref[...]
        expand = expand_ref[c]
        for k in range(tiles):
            scale = rows_ref[c, 4 * tiles + k:4 * tiles + k + 1]
            leaving = (gp_ref[c, k] + scale * value).astype(BF16)
            right = jnp.concatenate([gs_ref[c, span(k)], leaving], 0)
            up = dot(up_ref[span(k)], expand, 1, 0)
            gi_ref[span(k), cols] = (up * dot(left_ref[span(k)], right, 1, 0)).astype(BF16)
            acc_ref[gw, span(k)] += dot(xs_ref[c, span(k)], leaving, 1, 1)

    @pl.when(i == 2 * groups)
    def _():
        row = lax.broadcasted_iota(jnp.int32, (TILE, TILE), 0)
        col = lax.broadcasted_iota(jnp.int32, (TILE, TILE), 1)
        for k in range(tiles):
            weights = jnp.where(col >= row, raw_ref[span(k)], 0.0).astype(BF16)
            acc_ref[gw, span(k)] += dot(weights, r_ref[span(k)], 1, 0)
            acc_ref[gr, span(k)] += dot(weights, w_ref[span(k)], 0, 0)
        ring.start()

    @pl.when(i == 2 * groups + 1)
    def _():
        ring.join()

    @pl.when(i == 2 * groups + 3)
    def _():
        early = ring.total()

        @pl.when(odd == 1)
        def _():
            or_ref[...] = early

        @pl.when(odd == 0)
        def _():
            ow_ref[...] = early

    @pl.when(i == 3 * groups - 1)
    def _():
        ring2.start()
        ring2.join()
        late = ring2.total()

        @pl.when(odd == 1)
        def _():
            ow_ref[...] = late

        @pl.when(odd == 0)
        def _():
            or_ref[...] = late

        ring.drain()
        ring2.drain()
        ratio.wait_send()
        for n in range(groups):
            swap(n).wait_send()

            @pl.when(has_prev)
            def _():
                hand(n).wait_send()

            @pl.when(has_next)
            def _():
                forward(n).wait_send()


class Ring:
    def __init__(self, source, near, half, far, sa, ra, sb, rb):
        self.me = lax.axis_index("head")
        self.chips = lax.axis_size("head") // 2
        self.core = lax.rem(self.me, 2)
        self.chip = self.me // 2
        self.mate = self.me + 1 - 2 * self.core
        self.order = list(range(1, self.chips)) + [0]
        self.size = near.shape[1]
        self.source, self.near, self.half, self.far = source, near, half, far
        self.sems = sa, ra, sb, rb

    def peer(self, d):
        return 2 * lax.rem(self.chip + d, self.chips) + self.core

    def greet(self, barrier):
        pl.semaphore_signal(barrier, 1, device_id={"head": self.mate}, device_id_type=MESH)
        for d in range(1, self.chips):
            pl.semaphore_signal(barrier, 1, device_id={"head": self.peer(d)}, device_id_type=MESH)

    def block(self, h):
        return pl.ds(pl.multiple_of(h * self.size, self.size), self.size)

    def swap(self, d):
        sa, ra, _, _ = self.sems
        at = self.peer(d) + 1 - 2 * self.core
        return pltpu.make_async_remote_copy(
            self.source.at[self.block(at)], self.near.at[d], sa.at[d], ra.at[d],
            device_id={"head": self.mate}, device_id_type=MESH)

    def cross(self, d):
        _, _, sb, rb = self.sems
        return pltpu.make_async_remote_copy(
            self.half.at[d], self.far.at[d], sb.at[d], rb.at[d],
            device_id={"head": self.peer(d)}, device_id_type=MESH)

    def start(self):
        for d in self.order:
            self.swap(d).start()

    def join(self):
        for d in self.order:
            self.swap(d).wait_recv()
            self.half[d] = self.near[d] + self.source[self.block(self.peer(d))]
            if d:
                self.cross(d).start()

    def total(self):
        total = self.half[0]
        for d in range(1, self.chips):
            self.cross(d).wait_recv()
            total = total + self.far[d]
        return total.astype(BF16)

    def drain(self):
        for d in self.order:
            self.swap(d).wait_send()
            if d:
                self.cross(d).wait_send()


def body(x, g, w, r, ld, head_count):
    tokens, width = x.shape
    heads = ld.shape[0]
    state = w.shape[1]
    tiles = tokens // TILE
    limit = 48 * 1024 * 1024
    shape = jax.ShapeDtypeStruct
    vmem = pl.BlockSpec(memory_space=pltpu.VMEM)
    sem = pltpu.SemaphoreType.DMA
    lanes = min(LANES, width)
    groups = width // lanes
    whole = lambda i: (0, 0)
    columns = pl.BlockSpec((tokens, lanes), lambda i: (0, jnp.minimum(i, groups - 1)))
    slabs = pltpu.VMEM((groups, state, lanes), F32)
    size = tokens // head_count
    chips = head_count // 2
    links = [pltpu.VMEM((chips, size, state), F32)] * 3
    grad_input, grad_write, grad_read = pl.pallas_call(
        functools.partial(layer_kernel, heads, groups),
        grid=(3 * groups,),
        in_specs=[columns, columns,
                  pl.BlockSpec((tokens, state), whole), pl.BlockSpec((tokens, state), whole),
                  pl.BlockSpec((heads, tokens), whole)],
        out_specs=[vmem, vmem, vmem],
        out_shape=[shape((tokens, width), BF16), shape((size, state), BF16),
                   shape((size, state), BF16)],
        scratch_shapes=[
            pltpu.VMEM((groups, 2 * heads, lanes), BF16),
            pltpu.VMEM((tokens, 2 * heads), BF16),
            pltpu.VMEM((tokens, 2 * heads), BF16),
            pltpu.VMEM((6 * tiles, 2 * heads), BF16),
            pltpu.VMEM((groups, 6 * tiles, lanes), F32),
            pltpu.VMEM((tokens, TILE + state), BF16),
            pltpu.VMEM((groups, tokens, lanes), BF16),
            pltpu.VMEM((groups, tokens, lanes), BF16),
            pltpu.VMEM((groups, tiles, state, lanes), F32),
            pltpu.VMEM((groups, tiles, state, lanes), F32),
            pltpu.VMEM((groups, 2, state, lanes), F32),
            slabs, slabs, slabs, slabs,
            pltpu.VMEM((state, lanes), F32),
            pltpu.VMEM((tokens, TILE), F32),
            pltpu.VMEM((8, heads), F32),
            pltpu.VMEM((8, heads), F32),
            pltpu.VMEM((2, tokens, state), F32),
        ] + links * 2 + [sem((groups,))] * 6 + [sem] * 2 + [sem((chips,))] * 8,
        compiler_params=pltpu.CompilerParams(
            collective_id=0, has_side_effects=True, vmem_limit_bytes=limit),
        name="layer",
    )(x, g, w, r, ld)
    return grad_input, grad_write, grad_read


def solution(mesh):
    return jax.shard_map(
        functools.partial(body, head_count=mesh.shape["head"]),
        mesh=mesh,
        in_specs=(
            P("seq", "head"),
            P("seq", "head"),
            P("seq", None),
            P("seq", None),
            P("head", "seq"),
        ),
        out_specs=(P("seq", "head"), P(("seq", "head"), None), P(("seq", "head"), None)),
        check_vma=False,
    )
```

```python
import functools
import jax
import jax.numpy as jnp
from jax import lax
from jax.experimental import pallas as pl
from jax.experimental.pallas import tpu as pltpu
from jax.sharding import PartitionSpec as P

TILE = 128
MID = TILE // 2 - 1
LANES = 256
MESH = pl.DeviceIdType.MESH
F32 = jnp.float32
BF16 = jnp.bfloat16


def dot(a, b, ca, cb):
    return lax.dot_general(a, b, (((ca,), (cb,)), ((), ())), preferred_element_type=F32)


def pieces(value, count, axis):
    parts = []
    for _ in range(count):
        part = value.astype(BF16)
        parts.append(part)
        value = value - part.astype(F32)
    return jnp.concatenate(parts, axis=axis)


def fill_expand(expand_ref, heads):
    groups, rows, lanes = expand_ref.shape
    size = groups * lanes // heads
    row = lax.broadcasted_iota(jnp.int32, (rows, lanes), 0)
    col = lax.broadcasted_iota(jnp.int32, (rows, lanes), 1)
    for c in range(groups):
        low = (row % heads) * size - c * lanes
        expand_ref[c] = jnp.where((col >= low) & (col < low + size), 1.0, 0.0).astype(BF16)


def fill_decays(ld_ref, up_ref, down_ref, ends_ref, dec_ref):
    tokens = ld_ref.shape[1]
    tiles = tokens // TILE
    row = lax.broadcasted_iota(jnp.int32, (TILE, TILE), 0)
    col = lax.broadcasted_iota(jnp.int32, (TILE, TILE), 1)
    rel = jnp.where(col <= row, 1.0, 0.0) - jnp.where(col <= MID, 1.0, 0.0)
    rel = jnp.concatenate([rel.astype(BF16)] * 3, 1)
    for k in range(tiles):
        span = slice(k * TILE, (k + 1) * TILE)
        value = dot(rel, pieces(ld_ref[:, span], 3, 1), 1, 1)
        up_ref[span] = pieces(jnp.exp(-value), 2, 1)
        down_ref[span] = pieces(jnp.exp(value), 2, 1)
    logs = pieces(ld_ref[...], 3, 1)
    tile = lax.broadcasted_iota(jnp.int32, (tiles, tokens), 0)
    token = lax.broadcasted_iota(jnp.int32, (tiles, tokens), 1)
    low, mid, high = tile * TILE, tile * TILE + MID, (tile + 1) * TILE
    sets = [
        (token >= low) & (token <= mid),
        (token > mid) & (token < high),
        (token >= low) & (token < high),
        token <= mid,
        token > mid,
        token >= 0,
    ]
    for n, chosen in enumerate(sets):
        marks = jnp.where(chosen, 1.0, 0.0).astype(BF16)
        value = dot(jnp.concatenate([marks] * 3, 1), logs, 1, 1)
        ends_ref[n * tiles:(n + 1) * tiles] = pieces(jnp.exp(value), 2, 1)
    dec_ref[...] = jnp.broadcast_to(jnp.exp(value)[:1], dec_ref.shape)


def layer_kernel(heads, groups, x_ref, g_ref, w_ref, r_ref, ld_ref, gi_ref, ow_ref, or_ref,
                 expand_ref, up_ref, down_ref, ends_ref, rows_ref, left_ref, xs_ref, gs_ref,
                 sp_ref, gp_ref, loc_ref, got, prior, passed, theirs, val_ref, raw_ref, dec_ref, gotdec,
                 acc_ref, near, half, far, near2, half2, far2, sa, ra, sb, rb, sc, rc, sd, rd,
                 sn, rn, sf, rf, sn2, rn2, sf2, rf2):
    i = pl.program_id(0)
    me = lax.axis_index("seq")
    count = lax.axis_size("seq")
    tokens, lanes = x_ref.shape
    state = w_ref.shape[1]
    tiles = tokens // TILE
    odd = lax.rem(me, 2)
    partner = me + 1 - 2 * odd
    step = 4 * odd - 2
    nxt, prv, fed = me + step, me - step, partner + step
    has_next = (nxt >= 0) & (nxt < count)
    has_prev = (prv >= 0) & (prv < count)
    partner_prev = (fed >= 0) & (fed < count)
    mine, other = 1 - odd, odd
    gw, gr = odd, 1 - odd
    ring = Ring(acc_ref.at[0], near, half, far, sn, rn, sf, rf)
    ring2 = Ring(acc_ref.at[1], near2, half2, far2, sn2, rn2, sf2, rf2)
    ratio = pltpu.make_async_remote_copy(
        dec_ref, gotdec, sd, rd, device_id={"seq": partner}, device_id_type=MESH)
    c = lax.rem(i, groups)
    phase = i // groups
    cols = pl.ds(pl.multiple_of(c * lanes, lanes), lanes)

    def span(k):
        return slice(k * TILE, (k + 1) * TILE)

    def swap(c):
        return pltpu.make_async_remote_copy(
            loc_ref.at[c, other], got.at[c], sa.at[c], ra.at[c],
            device_id={"seq": partner}, device_id_type=MESH)

    def forward(c):
        return pltpu.make_async_remote_copy(
            passed.at[c], prior.at[c], sb.at[c], rb.at[c],
            device_id={"seq": nxt}, device_id_type=MESH)

    def hand(c):
        return pltpu.make_async_remote_copy(
            prior.at[c], theirs.at[c], sc.at[c], rc.at[c],
            device_id={"seq": partner}, device_id_type=MESH)

    @pl.when(i == 0)
    def _():
        barrier = pltpu.get_barrier_semaphore()
        pl.semaphore_signal(barrier, 1, device_id={"seq": partner}, device_id_type=MESH)

        @pl.when(has_next)
        def _():
            pl.semaphore_signal(barrier, 1, device_id={"seq": nxt}, device_id_type=MESH)

        @pl.when(has_prev)
        def _():
            pl.semaphore_signal(barrier, 1, device_id={"seq": prv}, device_id_type=MESH)

        acc_ref[...] = jnp.zeros_like(acc_ref)
        val_ref[...] = jnp.zeros_like(val_ref)
        fill_expand(expand_ref, heads)
        fill_decays(ld_ref, up_ref, down_ref, ends_ref, dec_ref)
        ring.greet(barrier)
        peers = ring.chips + 1 + has_next.astype(jnp.int32) + has_prev.astype(jnp.int32)
        pl.semaphore_wait(barrier, peers)
        ratio.start()

    @pl.when(phase == 0)
    def _():
        expand = expand_ref[c]
        rows = dot(ends_ref[...], expand, 1, 0)
        rows_ref[c] = rows
        xs = (x_ref[...].astype(F32) * dot(up_ref[...], expand, 1, 0)).astype(BF16)
        gs = (g_ref[...].astype(F32) * dot(down_ref[...], expand, 1, 0)).astype(BF16)
        xs_ref[c] = xs
        gs_ref[c] = gs
        carry = jnp.zeros((state, lanes), F32)
        for k in range(tiles):
            start, end, whole = (rows[n * tiles + k:n * tiles + k + 1] for n in range(3))
            sp_ref[c, k] = start * carry
            carry = whole * carry + end * dot(w_ref[span(k)], xs[span(k)], 0, 0)
        loc_ref[c, 0] = carry
        carry = jnp.zeros((state, lanes), F32)
        for k in reversed(range(tiles)):
            start, end, whole = (rows[n * tiles + k:n * tiles + k + 1] for n in range(3))
            gp_ref[c, k] = end * carry
            carry = whole * carry + start * dot(r_ref[span(k)], gs[span(k)], 0, 0)
        loc_ref[c, 1] = carry
        swap(c).start()

    @pl.when(i == groups - 1)
    def _():
        ratio.wait_recv()
        row = lax.broadcasted_iota(jnp.int32, (TILE, TILE), 0)
        col = lax.broadcasted_iota(jnp.int32, (TILE, TILE), 1)
        for k in range(tiles):
            pairs = jnp.where(col >= row, dot(w_ref[span(k)], r_ref[span(k)], 1, 1), 0.0)
            left_ref[span(k), :TILE] = pairs.astype(BF16)
            left_ref[span(k), TILE:] = w_ref[span(k)]
        raw_ref[...] = jnp.zeros_like(raw_ref)

    @pl.when(phase == 1)
    def _():
        swap(c).wait_recv()
        own = rows_ref[c, 5 * tiles:5 * tiles + 1]
        partners = dot(pieces(gotdec[...], 2, 1), expand_ref[c], 1, 0)[0:1]
        summed = own * got[c] + loc_ref[c, mine]

        @pl.when(has_prev)
        def _():
            forward(c).wait_recv()
            hand(c).start()
            passed[c] = (own * partners) * prior[c] + summed
            val_ref[...] = partners * prior[c] + got[c]

        @pl.when(jnp.logical_not(has_prev))
        def _():
            passed[c] = summed
            val_ref[...] = got[c]

        @pl.when(has_next)
        def _():
            forward(c).start()

        for k in range(tiles):
            raw_ref[span(k)] += dot(xs_ref[c, span(k)], gs_ref[c, span(k)], 1, 1)

    @pl.when(phase == 2)
    def _():
        @pl.when(partner_prev)
        def _():
            hand(c).wait_recv()
            val_ref[...] = theirs[c]

        @pl.when(jnp.logical_not(partner_prev))
        def _():
            val_ref[...] = jnp.zeros_like(val_ref)

    @pl.when(phase == jnp.where(odd == 1, 1, jnp.where(partner_prev, 2, 0)))
    def _():
        value = val_ref[...]
        for k in range(tiles):
            scale = rows_ref[c, 3 * tiles + k:3 * tiles + k + 1]
            entering = (sp_ref[c, k] + scale * value).astype(BF16)
            acc_ref[gr, span(k)] += dot(gs_ref[c, span(k)], entering, 1, 1)

    @pl.when(phase == jnp.where((odd == 1) & partner_prev, 2, 1))
    def _():
        value = val_ref[...]
        value = jnp.where((odd == 1) & (phase == 1), jnp.zeros_like(value), value)
        expand = expand_ref[c]
        for k in range(tiles):
            scale = rows_ref[c, 4 * tiles + k:4 * tiles + k + 1]
            leaving = (gp_ref[c, k] + scale * value).astype(BF16)
            right = jnp.concatenate([gs_ref[c, span(k)], leaving], 0)
            up = dot(up_ref[span(k)], expand, 1, 0)
            gi_ref[span(k), cols] = (up * dot(left_ref[span(k)], right, 1, 0)).astype(BF16)
            acc_ref[gw, span(k)] += dot(xs_ref[c, span(k)], leaving, 1, 1)

    @pl.when(i == 2 * groups)
    def _():
        row = lax.broadcasted_iota(jnp.int32, (TILE, TILE), 0)
        col = lax.broadcasted_iota(jnp.int32, (TILE, TILE), 1)
        for k in range(tiles):
            weights = jnp.where(col >= row, raw_ref[span(k)], 0.0).astype(BF16)
            acc_ref[gw, span(k)] += dot(weights, r_ref[span(k)], 1, 0)
            acc_ref[gr, span(k)] += dot(weights, w_ref[span(k)], 0, 0)
        ring.start()

    @pl.when(i == 2 * groups + 1)
    def _():
        ring.join()

    @pl.when(i == 2 * groups + 3)
    def _():
        early = ring.total()

        @pl.when(odd == 1)
        def _():
            or_ref[...] = early

        @pl.when(odd == 0)
        def _():
            ow_ref[...] = early

    @pl.when(i == 3 * groups - 1)
    def _():
        ring2.start()
        ring2.join()
        late = ring2.total()

        @pl.when(odd == 1)
        def _():
            ow_ref[...] = late

        @pl.when(odd == 0)
        def _():
            or_ref[...] = late

        ring.drain()
        ring2.drain()
        ratio.wait_send()
        for n in range(groups):
            swap(n).wait_send()

            @pl.when(has_prev)
            def _():
                hand(n).wait_send()

            @pl.when(has_next)
            def _():
                forward(n).wait_send()


class Ring:
    def __init__(self, source, near, half, far, sa, ra, sb, rb):
        self.me = lax.axis_index("head")
        self.chips = lax.axis_size("head") // 2
        self.core = lax.rem(self.me, 2)
        self.chip = self.me // 2
        self.mate = self.me + 1 - 2 * self.core
        self.order = list(range(1, self.chips)) + [0]
        self.size = near.shape[1]
        self.source, self.near, self.half, self.far = source, near, half, far
        self.sems = sa, ra, sb, rb

    def peer(self, d):
        return 2 * lax.rem(self.chip + d, self.chips) + self.core

    def greet(self, barrier):
        pl.semaphore_signal(barrier, 1, device_id={"head": self.mate}, device_id_type=MESH)
        for d in range(1, self.chips):
            pl.semaphore_signal(barrier, 1, device_id={"head": self.peer(d)}, device_id_type=MESH)

    def block(self, h):
        return pl.ds(pl.multiple_of(h * self.size, self.size), self.size)

    def swap(self, d):
        sa, ra, _, _ = self.sems
        at = self.peer(d) + 1 - 2 * self.core
        return pltpu.make_async_remote_copy(
            self.source.at[self.block(at)], self.near.at[d], sa.at[d], ra.at[d],
            device_id={"head": self.mate}, device_id_type=MESH)

    def cross(self, d):
        _, _, sb, rb = self.sems
        return pltpu.make_async_remote_copy(
            self.half.at[d], self.far.at[d], sb.at[d], rb.at[d],
            device_id={"head": self.peer(d)}, device_id_type=MESH)

    def start(self):
        for d in self.order:
            self.swap(d).start()

    def join(self):
        for d in self.order:
            self.swap(d).wait_recv()
            self.half[d] = self.near[d] + self.source[self.block(self.peer(d))]
            if d:
                self.cross(d).start()

    def total(self):
        total = self.half[0]
        for d in range(1, self.chips):
            self.cross(d).wait_recv()
            total = total + self.far[d]
        return total.astype(BF16)

    def drain(self):
        for d in self.order:
            self.swap(d).wait_send()
            if d:
                self.cross(d).wait_send()


def body(x, g, w, r, ld, head_count):
    tokens, width = x.shape
    heads = ld.shape[0]
    state = w.shape[1]
    tiles = tokens // TILE
    limit = 48 * 1024 * 1024
    shape = jax.ShapeDtypeStruct
    vmem = pl.BlockSpec(memory_space=pltpu.VMEM)
    sem = pltpu.SemaphoreType.DMA
    lanes = min(LANES, width)
    groups = width // lanes
    whole = lambda i: (0, 0)
    columns = pl.BlockSpec((tokens, lanes), lambda i: (0, jnp.minimum(i, groups - 1)))
    slabs = pltpu.VMEM((groups, state, lanes), F32)
    size = tokens // head_count
    chips = head_count // 2
    links = [pltpu.VMEM((chips, size, state), F32)] * 3
    grad_input, grad_write, grad_read = pl.pallas_call(
        functools.partial(layer_kernel, heads, groups),
        grid=(3 * groups,),
        in_specs=[columns, columns,
                  pl.BlockSpec((tokens, state), whole), pl.BlockSpec((tokens, state), whole),
                  pl.BlockSpec((heads, tokens), whole)],
        out_specs=[vmem, vmem, vmem],
        out_shape=[shape((tokens, width), BF16), shape((size, state), BF16),
                   shape((size, state), BF16)],
        scratch_shapes=[
            pltpu.VMEM((groups, 2 * heads, lanes), BF16),
            pltpu.VMEM((tokens, 2 * heads), BF16),
            pltpu.VMEM((tokens, 2 * heads), BF16),
            pltpu.VMEM((6 * tiles, 2 * heads), BF16),
            pltpu.VMEM((groups, 6 * tiles, lanes), F32),
            pltpu.VMEM((tokens, TILE + state), BF16),
            pltpu.VMEM((groups, tokens, lanes), BF16),
            pltpu.VMEM((groups, tokens, lanes), BF16),
            pltpu.VMEM((groups, tiles, state, lanes), F32),
            pltpu.VMEM((groups, tiles, state, lanes), F32),
            pltpu.VMEM((groups, 2, state, lanes), F32),
            slabs, slabs, slabs, slabs,
            pltpu.VMEM((state, lanes), F32),
            pltpu.VMEM((tokens, TILE), F32),
            pltpu.VMEM((8, heads), F32),
            pltpu.VMEM((8, heads), F32),
            pltpu.VMEM((2, tokens, state), F32),
        ] + links * 2 + [sem((groups,))] * 6 + [sem] * 2 + [sem((chips,))] * 8,
        compiler_params=pltpu.CompilerParams(
            collective_id=0, has_side_effects=True, vmem_limit_bytes=limit),
        name="layer",
    )(x, g, w, r, ld)
    return grad_input, grad_write, grad_read


def solution(mesh):
    return jax.shard_map(
        functools.partial(body, head_count=mesh.shape["head"]),
        mesh=mesh,
        in_specs=(
            P("seq", "head"),
            P("seq", "head"),
            P("seq", None),
            P("seq", None),
            P("head", "seq"),
        ),
        out_specs=(P("seq", "head"), P(("seq", "head"), None), P(("seq", "head"), None)),
        check_vma=False,
    )
```
